512 devices in a mesh: seq: 128 (over y_hi, z, x), book: 4 (over y_lo, core).
Axes of the slice: x: 4, y: 8 (y_hi: 4, y_lo: 2; y = y_hi * 2 + y_lo), z: 8, core: 2. Of those that a mesh axis runs over, the one named last changes fastest.
Arguments:
- features: bfloat16 [4, 16384, 512], P('book', 'seq'), may hold values from -6 to 6
- lengths: int32 [4, 8], P('book'), may hold values from 1 to 4096, 16384 in all within a row
- owner: int32 [4, 16384, 1], P('book', 'seq'), may hold values from 0 to 127; in each aligned block of 128 rows (0 to 127, 128 to 255, ..., all dimensions but the last counted through in order) at most 2 rows name the same one
- w_enc: bfloat16 [3, 512, 256], replicated, may hold values from -0.15625 to 0.15625
- w_in: bfloat16 [256, 2048], P(None, ('seq', 'book')), may hold values from -0.375 to 0.375
- gain: float32 [2048], replicated, may hold values from 0.1 to 1.9
- cotangent: bfloat16 [4, 32768, 2048], P('book', 'seq'), may hold values from -24 to 24
Outputs:
- grad_features: bfloat16 [4, 16384, 512], P('book', 'seq')
- grad_w_enc: float32 [3, 512, 256], P(None, 'book')
- grad_w_in: float32 [256, 2048], P(None, ('seq', 'book'))
- grad_gain: float32 [2048], replicated
The draws below stay inside these ranges and needn't reach their ends.
Inputs may be any that keep to these rules, and one draw needn't show every extreme that they name: Of the 128 frames of one device's block no more than 2 have the same owner, and in some block exactly 2 do. The 8 lengths of a stream sum to 16384; the largest is 4096.
All inputs are finite; a program needn't handle non-finite values.
Results may differ from the reference program's by a relative error of at most 0.0095.
Values may be sent and summed in bfloat16 or wider, within the bound.
A program may use at most 64 MiB of HBM per device.

```python
import math
import jax
import jax.numpy as jnp
import numpy as np
from jax import lax

DM = 2048
C_IN = 512
LAT = 256
KW = 3
NB = 8
FR = 128
CAP = 2
TOTAL = 16384
SLOTS = 32768
N_SEQ = 128
N_BOOK = 4


def raised(result, stream_key, source, target, blocks, factor):
    owner, partner = [(jnp.arange(result.shape[dim]) // (result.shape[dim] // blocks)).reshape([-1 if axis == dim else 1 for axis in range(result.ndim)]) for dim in (source, target)]
    chosen = jax.random.permutation(stream_key, blocks)[partner]
    strong = (owner == chosen) | (owner == (partner + blocks // 2) % blocks)
    return jnp.where(strong, factor * result, result)


def level_of(rng, dims, split, low, high):
    def one(dim, shards_of):
        heights = jax.random.uniform(jax.random.fold_in(jax.random.fold_in(rng, 6), dim), (shards_of,), jnp.float32, low / len(split), high / len(split))
        return jnp.repeat(jnp.exp(heights), dims[dim] // shards_of).reshape((-1,) + (1,) * (len(dims) - dim - 1))

    loudness = one(*split[0])
    for cut in split[1:]:
        loudness = loudness * one(*cut)
    return loudness


def split_up(count, total, most, skew):
    loads = [(1 << 20) // math.isqrt(standing ** skew) + 1 for standing in range(2, count + 1)]
    rest, holding = total - most - (count - 1), [1] * (count - 1)
    while rest > 0:
        movable = [i for i in range(count - 1) if holding[i] < most]
        whole, left = sum([loads[i] for i in movable]), rest
        for i in movable:
            addition = min(most - holding[i], max(1, left * loads[i] // whole), rest)
            holding[i] = holding[i] + addition
            rest = rest - addition
    return np.array([most] + holding)


def uneven_parts(rng, count, total, limit, skew):
    if count == 2:
        one = jax.random.randint(rng, (), max(1, total - limit), min(limit, total - 1) + 1)
        return jnp.stack([one, total - one])
    tallies = jnp.asarray(split_up(count, total, limit, skew), jnp.int32)
    couples = (count - 1) // 2
    giver, sink = tallies[1:1 + 2 * couples:2], tallies[2:2 + 2 * couples:2]
    margin = jnp.minimum(giver - 1, limit - sink)
    passed = jax.random.randint(jax.random.fold_in(rng, 1), (couples,), 0, 1 << 20) % (margin + 1)
    tallies = tallies.at[1:1 + 2 * couples:2].set(giver - passed).at[2:2 + 2 * couples:2].set(sink + passed)
    return tallies[jax.random.permutation(jax.random.fold_in(rng, 2), count)]


def assign_block(rng, own, number, rows, count, top, reach, skew):
    order = jax.random.permutation(rng, count)
    crowded, ordinary = load_shares(count, rows * top, reach, skew, True), load_shares(count, rows * top, reach, skew, False)
    places = jnp.arange(count)

    def named(tallies, offset_by):
        used = int((tallies > 0).sum())
        fixed = max(1, used // 4)
        moved = fixed + (places - fixed + offset_by * (used - fixed)) % max(1, count - fixed)
        return jnp.zeros((count,), jnp.int32).at[order[jnp.where(places < fixed, places, moved)]].set(jnp.asarray(tallies, jnp.int32))

    tallies = jnp.where(number % 4 == 0, named(crowded, number // 4), named(ordinary, number - number // 4 - 1))
    mixed = jax.random.permutation(jax.random.fold_in(own, 3), count)
    source_of, sink = mixed[0:count // 2 * 2:2], mixed[1:count // 2 * 2:2]
    room = jnp.minimum(tallies[source_of] - 1, reach - tallies[sink]) // 2
    room = jnp.where((source_of == order[0]) | (sink == order[0]) | (tallies[sink] == 0), 0, jnp.maximum(room, 0))
    moved = jax.random.randint(jax.random.fold_in(own, 4), (count // 2,), 0, 1 << 20) % (room + 1)
    tallies = tallies.at[source_of].add(-moved).at[sink].add(moved)
    labels = jnp.searchsorted(jnp.cumsum(tallies), jnp.arange(rows * top), side="right").astype(jnp.int32)
    listing = labels.reshape(top, rows).T
    listing = listing[jax.random.permutation(jax.random.fold_in(own, 1), rows)]
    offset_by = jax.random.randint(jax.random.fold_in(own, 2), (rows, 1), 0, top)
    return jnp.take_along_axis(listing, (jnp.arange(top)[None, :] + offset_by) % top, axis=1)


def load_shares(count, total, bound, skew, full):
    portions = [(1 << 20) // math.isqrt(rank ** skew) + 1 for rank in range(1, count + 1)]
    largest = bound if full else min(bound, max(-(-total // count), total * portions[0] // sum(portions)))
    least = 1 if total - largest >= count - 1 else 0
    counts, rest = [largest] + [least] * (count - 1), total - largest - least * (count - 1)
    while rest > 0:
        movable = [i for i in range(1, count) if counts[i] < largest] or [i for i in range(1, count) if counts[i] < bound]
        whole, budget = sum([portions[i] for i in movable]), rest
        for i in movable:
            addition = min(bound - counts[i], max(1, budget * portions[i] // whole), rest)
            counts[i] = counts[i] + addition
            rest = rest - addition
    return np.array(counts)


def gaussian(own_key, extent, width, most, shards=(), kind=jnp.bfloat16):
    values = width * jax.random.normal(own_key, extent, jnp.float32)
    if shards:
        values = values * level_of(own_key, extent, shards, -0.22, 0.18)
    return jnp.clip(values, -most, most).astype(kind)


def noise_with(stream_key, shape, width, most, shards, heavy, kind=jnp.bfloat16):
    drawn = width * jax.random.normal(stream_key, shape, jnp.float32)
    if shards:
        drawn = drawn * level_of(stream_key, shape, shards, -0.22, 0.18)
    return jnp.clip(raised(drawn, jax.random.fold_in(stream_key, 3), *heavy), -most, most).astype(kind)


def setup_inputs(seed: int = 0) -> dict:
    arg_keys = jax.random.split(jax.random.key(seed), 8)
    features = gaussian(arg_keys[0], (N_BOOK, TOTAL, C_IN), 1.0, 6.0, ((0, 4), (1, 128)))
    lengths = jax.vmap(lambda own: uneven_parts(own, NB, TOTAL, TOTAL // 4, 2))(jax.random.split(arg_keys[1], N_BOOK)).reshape((N_BOOK, NB)).astype(jnp.int32)
    owner_keys = jax.random.split(jax.random.fold_in(arg_keys[2], 1), N_BOOK * TOTAL // FR)
    owner_turns = jax.random.permutation(jax.random.fold_in(arg_keys[2], 3), N_BOOK * TOTAL // FR)
    owner = jax.vmap(lambda own, number: assign_block(jax.random.fold_in(arg_keys[2], 2), own, number, FR, N_SEQ, 1, CAP, 2))(owner_keys, owner_turns).reshape((N_BOOK, TOTAL, 1))
    w_enc = gaussian(arg_keys[3], (KW, C_IN, LAT), (KW * C_IN) ** -0.5, 0.15625)
    w_in = gaussian(arg_keys[4], (LAT, DM), LAT ** -0.5, 0.375, ((1, 512),))
    gain = jnp.clip(1.0 + 0.18 * jax.random.normal(arg_keys[5], (DM,), jnp.float32), 0.1, 1.9)
    cotangent = noise_with(arg_keys[6], (N_BOOK, SLOTS, DM), 1.0, 24.0, ((0, 4), (1, 128)), (1, 2, 128, 5.5))
    return dict(features=features, lengths=lengths, owner=owner, w_enc=w_enc, w_in=w_in, gain=gain, cotangent=cotangent)


def book_starts(book_lengths, position):
    starts = jnp.cumsum(book_lengths) - book_lengths
    return lax.optimization_barrier(jnp.max(jnp.where(starts[None, :] <= position[:, None], starts[None, :], 0), axis=1))

def stream_grads(feature_rows, book_lengths, owner_rows, cotangent_rows, w_enc, w_full, gain):
    total_frames, channels = feature_rows.shape
    latent_width = w_enc.shape[2]
    frames = total_frames // N_SEQ
    capacity = max(2, frames // N_SEQ + 1)
    position = jnp.arange(total_frames, dtype=jnp.int32)
    start_of = book_starts(book_lengths, position)
    feats_wide = feature_rows.astype(jnp.float32)
    activated = jax.nn.elu(feats_wide).astype(jnp.bfloat16)
    tap_inputs = []
    tap_masks = []
    for offset in range(KW):
        shifted = jnp.concatenate([jnp.zeros((offset, channels), jnp.bfloat16), activated[:total_frames - offset]], axis=0)
        valid_tap = position - offset >= start_of
        tap_masks.append(valid_tap)
        tap_inputs.append(jnp.where(valid_tap[:, None], shifted, jnp.zeros_like(shifted)))
    stacked = jnp.concatenate(tap_inputs, axis=1)
    latent = jnp.dot(stacked, w_enc.reshape(KW * channels, latent_width), preferred_element_type=jnp.float32).astype(jnp.bfloat16)
    owner_rank = owner_rows[:, 0]
    one_hot = (owner_rank.reshape(N_SEQ, frames)[:, :, None] == jnp.arange(N_SEQ, dtype=jnp.int32)[None, None, :]).astype(jnp.int32)
    slot_rank = lax.optimization_barrier(jnp.sum((jnp.cumsum(one_hot, axis=1) - one_hot) * one_hot, axis=2)).reshape(total_frames)
    slot_index = (owner_rank * (N_SEQ * capacity) + position // frames * capacity + slot_rank).astype(jnp.int32)
    grad_out = cotangent_rows[slot_index].astype(jnp.float32)
    hidden = jnp.dot(latent, w_full, preferred_element_type=jnp.float32)
    inv_rms = lax.rsqrt(lax.optimization_barrier(jnp.mean(hidden * hidden, axis=1, keepdims=True)) + 1e-05)
    normed = hidden * inv_rms
    gain_term = grad_out * gain[None, :]
    hidden_grad = (inv_rms * (gain_term - normed * lax.optimization_barrier(jnp.mean(gain_term * normed, axis=1, keepdims=True)))).astype(jnp.bfloat16)
    latent_grad = jnp.dot(hidden_grad, w_full.T, preferred_element_type=jnp.float32).astype(jnp.bfloat16)
    w_in_grad = jnp.dot(latent.T, hidden_grad, preferred_element_type=jnp.float32)
    gain_grad = lax.optimization_barrier(jnp.sum(grad_out * normed, axis=0))
    activ_grad = jnp.zeros((total_frames, channels), jnp.float32)
    for offset in range(KW):
        masked = jnp.where(tap_masks[offset][:, None], latent_grad, jnp.zeros_like(latent_grad))
        moved = jnp.concatenate([masked[offset:], jnp.zeros((offset, latent_width), jnp.bfloat16)], axis=0)
        activ_grad = activ_grad + jnp.dot(moved, w_enc[offset].T, preferred_element_type=jnp.float32)
    kernel_grad = jnp.dot(stacked.T, latent_grad, preferred_element_type=jnp.float32).reshape(KW, channels, latent_width)
    slope = jnp.where(feats_wide > 0, 1.0, jnp.exp(feats_wide))
    feature_grad = (slope * activ_grad).astype(jnp.bfloat16)
    return (feature_grad, kernel_grad, w_in_grad, gain_grad)

def reference(features, lengths, owner, w_enc, w_in, gain, cotangent):

    def per_stream(stream_args):
        return stream_grads(stream_args[0], stream_args[1], stream_args[2], stream_args[3], w_enc, w_in, gain)
    feature_grad, kernel_grad, w_in_grad, gain_grad = lax.map(per_stream, (features, lengths, owner, cotangent))
    return (feature_grad, lax.optimization_barrier(jnp.sum(kernel_grad, axis=0)), lax.optimization_barrier(jnp.sum(w_in_grad, axis=0)), lax.optimization_barrier(jnp.sum(gain_grad, axis=0)))
```

```python
import functools

import jax
import jax.numpy as jnp
from jax import lax
from jax.experimental import pallas as pl
from jax.experimental.pallas import tpu as pltpu
from jax.sharding import PartitionSpec as P

NX, NZ, NH, NL, NC = 4, 8, 4, 2, 2
NY = NH * NL
NSEQ = NX * NZ * NH
FR, CH, LAT, DM, CAP = 128, 512, 256, 2048, 2
ROWS = NSEQ * CAP
EPS = 1e-05
BF, F32, I32 = jnp.bfloat16, jnp.float32, jnp.int32
NT = (((1,), (1,)), ((), ()))
NN = (((1,), (0,)), ((), ()))
TN = (((0,), (0,)), ((), ()))
NSEM = 144


def dot(a, b, dims):
    return lax.dot_general(a, b, dims, preferred_element_type=F32)


def kernel(
    feat_ref, lens_ref, owner_ref, wpad_ref, gain_ref, wenc_any, cot_any,
    gf_ref, ge_ref, gw_ref, gg_ref,
    cot, wenc, ext, edge_s, edge_r, win, bkr, wf,
    a_out, r1, r2, pbuf, r3, arr2, hid, hg,
    lbuf, b1, c2, b2, b3, lext, edge2_s, edge2_r,
    as0, ar0, aown, s0, axr, s1, azr, s2, ayr, s3, acr,
    gs, gcr, gxr, gzr, gyr, gacc,
    efull, es0, er0, exs, exr, ezs, ezr, eys, eyr, gz, gx,
    send_sem, recv_sem, local_sem,
):
    seq, book = lax.axis_index("seq"), lax.axis_index("book")
    h, z, x = seq // (NZ * NX), (seq // NX) % NZ, seq % NX
    l, c = book // NC, book % NC
    y = h * NL + l
    other = 1 - c

    def dev(h=h, z=z, x=x, l=l, c=c):
        return ((h * NZ + z) * NX + x, l * NC + c)

    def dev_x(p):
        return dev(x=p)

    def dev_z(p):
        return dev(z=p)

    def dev_h(p):
        return dev(h=p)

    def dev_y(p):
        return dev(h=p // NL, l=p % NL)

    def dev_c(p):
        return dev(c=p)

    def dev_b(p):
        return dev(l=p // NC, c=p % NC)

    right = (lax.rem(seq + 1, NSEQ), book)
    left = (lax.rem(seq + NSEQ - 1, NSEQ), book)

    count = [0]
    started = []

    def push(src, dst, to):
        k = count[0]
        count[0] += 1
        copy = pltpu.make_async_remote_copy(
            src_ref=src, dst_ref=dst, send_sem=send_sem.at[k], recv_sem=recv_sem.at[k],
            device_id=to, device_id_type=pl.DeviceIdType.MESH,
        )
        copy.start()
        started.append(copy)
        return copy

    def spread(n, me, src, dst, to):
        order = sorted(range(1, n), key=lambda d: -min(d, n - d))
        copies = []
        for d in order:
            p = lax.rem(me + d, n)
            copies.append(push(src(p), dst, to(p)))
        return copies

    def landed(copies):
        for copy in copies:
            copy.wait_recv()

    barrier = pltpu.get_barrier_semaphore()
    partners = [right, left]
    for n, me, to in ((NX, x, dev_x), (NZ, z, dev_z), (NY, y, dev_y)):
        for d in range(1, n):
            partners.append(to(lax.rem(me + d, n)))
    partners.append(dev_c(other))
    partners.append(dev(l=1 - l, c=other))
    for to in partners:
        pl.semaphore_signal(barrier, inc=1, device_id=to, device_id_type=pl.DeviceIdType.MESH)

    load_w = pltpu.make_async_copy(wenc_any, wenc, local_sem.at[0])
    load_c = pltpu.make_async_copy(cot_any, cot, local_sem.at[1])
    load_w.start()
    load_c.start()

    feats = feat_ref[...].astype(F32)
    low = jnp.minimum(feats, 0.0)
    act = jnp.where(feats > 0, feats, (jnp.exp(low) + 1.0) * jnp.tanh(0.5 * low))
    act = act.astype(BF)
    edge_s[...] = act[FR - 16 :]
    ext[pl.ds(8, FR), :] = act.astype(F32)

    pl.semaphore_wait(barrier, len(partners))

    edge = push(edge_s, edge_r, right)
    bk = []
    for dl, dc in ((1, 0), (1, 1), (0, 1)):
        to_l, to_c = lax.rem(l + dl, NL), lax.rem(c + dc, NC)
        bk.append(push(wpad_ref.at[to_c], bkr.at[book], dev(l=to_l, c=to_c)))
    bkr[book] = wpad_ref[c]

    eye = lax.broadcasted_iota(I32, (FR, FR), 0) == lax.broadcasted_iota(I32, (FR, FR), 1)
    before = lax.broadcasted_iota(I32, (FR, FR), 0) < lax.broadcasted_iota(I32, (FR, FR), 1)
    row = owner_ref[...].astype(F32)
    row_b = jnp.broadcast_to(row, (FR, FR))
    col = jnp.sum(jnp.where(eye, row_b, 0.0), axis=1, keepdims=True)
    same = jnp.where(before, jnp.where(jnp.broadcast_to(col, (FR, FR)) == row_b, 1.0, 0.0), 0.0)
    rank = jnp.sum(same, axis=0, keepdims=True).astype(I32)
    own = owner_ref[...]
    own_h, own_z, own_x = own >> 5, (own >> 2) & (NZ - 1), own & (NX - 1)
    slot_row = (((own_x * NZ + own_z) * NH + own_h) * CAP + rank).astype(F32)
    slot_col = jnp.sum(
        jnp.where(eye, jnp.broadcast_to(slot_row, (FR, FR)), 0.0), axis=1, keepdims=True
    )
    place_t = jnp.where(
        lax.broadcasted_iota(I32, (ROWS, FR), 0).astype(F32)
        == jnp.broadcast_to(slot_row, (ROWS, FR)), 1.0, 0.0,
    ).astype(BF)
    place = jnp.where(
        lax.broadcasted_iota(I32, (FR, ROWS), 1).astype(F32)
        == jnp.broadcast_to(slot_col, (FR, ROWS)), 1.0, 0.0,
    ).astype(BF)

    pos = seq * FR + lax.broadcasted_iota(I32, (FR, 1), 0)
    starts = []
    total = jnp.int32(0)
    for i in range(lens_ref.shape[1]):
        starts.append(total)
        total = total + lens_ref[0, i]

    def start_of(p):
        best = jnp.zeros_like(p)
        for s in starts:
            best = jnp.maximum(best, jnp.where(p >= s, s, 0))
        return best

    start_here = start_of(pos)
    masks = [jnp.where(pos - k >= start_here, 1.0, 0.0) for k in range(3)]
    back_masks = [masks[0]]
    for k in (1, 2):
        ok = jnp.where(pos >= start_of(pos + k), 1.0, 0.0)
        back_masks.append(ok * jnp.where(pos + k < NSEQ * FR, 1.0, 0.0))

    landed(bk)
    block = bkr[0].astype(F32)
    for i in range(1, 4):
        block = block + bkr[i].astype(F32)
    wf[c, h, z, x] = block.astype(BF)
    mine = wf.at[c, h, z, x]
    w_h = spread(NH, h, lambda p: mine, mine, dev_h)

    load_w.wait()
    edge.wait_recv()
    ext[pl.ds(0, 8), :] = edge_r[...].astype(F32)[8:]
    latent = None
    for k in range(3):
        w = (ext[pl.ds(8 - k, FR), :] * masks[k]).astype(BF)
        win[k] = w
        term = dot(w, wenc[k], NN)
        latent = term if latent is None else latent + term
    latent = latent.astype(BF)
    outgoing = dot(place_t, latent, NN)
    for i in range(NX * NZ):
        a_out[i // NZ, i % NZ] = outgoing[8 * i : 8 * i + 8].astype(BF)
    a_x = spread(NX, x, lambda p: a_out.at[p], r1.at[x], dev_x)
    r1[x] = a_out[x]

    landed(w_h)
    slab = wf.at[c, :, z, x]
    w_z = spread(NZ, z, lambda p: slab, slab, dev_z)

    landed(a_x)
    a_z = spread(NZ, z, lambda p: r1.at[:, p], r2.at[z], dev_z)
    r2[z] = r1[:, z]

    landed(w_z)
    slab = wf.at[c, :, :, x]
    w_x = spread(NX, x, lambda p: slab, slab, dev_x)
    w_c = [push(slab, slab, dev_c(other))]

    jj = lax.broadcasted_iota(I32, (ROWS, ROWS), 0)
    ii = lax.broadcasted_iota(I32, (ROWS, ROWS), 1)
    landed(a_z)
    rows_in = jnp.concatenate(
        [r2[i // NX, i % NX].astype(F32) for i in range(NX * NZ)], axis=0
    ).astype(BF)
    sent_from = ((jj >> 1) & 31) * 8 + (jj >> 6) * 2 + (jj & 1)
    perm = jnp.where(ii == sent_from, 1.0, 0.0).astype(BF)
    moved = dot(perm, rows_in, NN).astype(BF)
    for i in range(NH):
        pbuf[i] = moved[64 * i : 64 * i + 64]
    a_h = spread(NH, h, lambda p: pbuf.at[p], r3.at[h], dev_h)
    r3[h] = pbuf[h]

    order = sorted(range(1, NX), key=lambda d: -min(d, NX - d))
    for copy, d in sorted(zip(w_x, order), key=lambda cd: min(cd[1], NX - cd[1])):
        copy.wait_recv()
        part = wf.at[c, :, :, lax.rem(x + NX - d, NX)]
        w_c.append(push(part, part, dev_c(other)))

    landed(a_h)
    for i in range(NH):
        block = r3[i]
        arr2[0, pl.ds(64 * i, 64), :] = block[:, :128]
        arr2[1, pl.ds(64 * i, 64), :] = block[:, 128:]
    landed(w_c)
    load_c.wait()

    arrived = jnp.concatenate([arr2[0], arr2[1]], axis=1)
    for i in range(NH):
        w0 = wf[0, i].reshape(DM // NH, 128)
        w1 = wf[1, i].reshape(DM // NH, 128)
        wide = jnp.concatenate([w0, w1], axis=1)
        hid[:, i * (DM // NH) : (i + 1) * (DM // NH)] = dot(arrived, wide, NT)
    gain = gain_ref[...]
    gacc[...] = jnp.zeros_like(gacc)

    def norm_rows(i, carry):
        at = pl.ds(pl.multiple_of(i * 16, 16), 16)
        hidden = hid[at, :]
        grad = cot[at, :].astype(F32)
        inv = lax.rsqrt(jnp.mean(hidden * hidden, axis=1, keepdims=True) + EPS)
        normed = hidden * inv
        scaled = grad * gain
        mean = jnp.mean(scaled * normed, axis=1, keepdims=True)
        hg[at, :] = (inv * (scaled - normed * mean)).astype(BF)
        prod = grad * normed
        gacc[...] += prod[:8] + prod[8:]
        return carry

    lax.fori_loop(0, ROWS // 16, norm_rows, 0)

    back = None
    for i in range(NH):
        w0 = wf[0, i].reshape(DM // NH, 128)
        w1 = wf[1, i].reshape(DM // NH, 128)
        wide = jnp.concatenate([w0, w1], axis=1)
        term = dot(hg[:, i * (DM // NH) : (i + 1) * (DM // NH)], wide, NN)
        back = term if back is None else back + term
    back = back.astype(BF)
    for i in range(NH):
        lbuf[i] = back[64 * i : 64 * i + 64]
    l_h = spread(NH, h, lambda p: lbuf.at[p], b1.at[h], dev_h)
    b1[h] = lbuf[h]

    gs[0] = jnp.sum(gacc[...], axis=0, keepdims=True)
    g_c = [push(gs.at[0], gcr.at[c], dev_c(other))]
    gcr[c] = gs[0]
    for i in range(NH):
        at = slice(i * (DM // NH), (i + 1) * (DM // NH))
        as0[at, :] = dot(hg[:, at], arr2[other], TN).astype(BF)
    p_c = [push(as0, ar0, dev_c(other))]
    for i in range(NH):
        at = slice(i * (DM // NH), (i + 1) * (DM // NH))
        aown[at, :] = dot(hg[:, at], arr2[c], TN)

    landed(l_h)
    rows_in = jnp.concatenate([b1[i] for i in range(NH)], axis=0)
    sent_from = ((jj >> 1) & 3) * 64 + (jj >> 3) * 2 + (jj & 1)
    perm = jnp.where(ii == sent_from, 1.0, 0.0).astype(BF)
    moved = dot(perm, rows_in, NN)
    for i in range(NX * NZ):
        c2[i // NX, i % NX] = moved[8 * i : 8 * i + 8].astype(BF)
    l_z = spread(NZ, z, lambda p: c2.at[p], b2.at[z], dev_z)
    b2[z] = c2[z]

    landed(p_c)
    for i in range(NH):
        at = slice(i * (DM // NH), (i + 1) * (DM // NH))
        both = aown[at, :] + ar0[at, :].astype(F32)
        s0[i] = both.astype(BF).reshape(NZ, NX, 16, 128)
    p_x = spread(NX, x, lambda p: s0.at[:, :, p], axr.at[x], dev_x)
    axr[x] = s0[:, :, x]
    landed(g_c)
    gs[1] = gcr[0] + gcr[1]
    g_x = spread(NX, x, lambda p: gs.at[1], gxr.at[x], dev_x)
    gxr[x] = gs[1]

    landed(l_z)
    l_x = spread(NX, x, lambda p: b2.at[:, p], b3.at[x], dev_x)
    b3[x] = b2[:, x]

    landed(l_x)
    returned = jnp.concatenate(
        [b3[i // NZ, i % NZ].astype(F32) for i in range(NX * NZ)], axis=0
    ).astype(BF)
    lat_grad_wide = dot(place, returned, NN)
    lat_grad = lat_grad_wide.astype(BF)
    edge2_s[...] = lat_grad[:16]
    edge2 = push(edge2_s, edge2_r, left)
    for k in range(3):
        part = dot(win[k], lat_grad, TN)
        efull[k] = part
        for i in range(NL):
            for j in range(NC):
                at = (i * NC + j) * 128
                es0[j, k, i] = part[at : at + 128].astype(BF)
    e_c = [push(es0.at[other], er0, dev_c(other))]
    lext[pl.ds(0, FR), :] = lat_grad.astype(F32)

    landed(p_x)
    for i in range(NH):
        acc = axr[0, i].astype(F32)
        for j in range(1, NX):
            acc = acc + axr[j, i].astype(F32)
        s1[i] = acc.astype(BF)
    p_z = spread(NZ, z, lambda p: s1.at[:, p], azr.at[z], dev_z)
    azr[z] = s1[:, z]
    landed(g_x)
    acc = gxr[0]
    for j in range(1, NX):
        acc = acc + gxr[j]
    gs[2] = acc
    g_z = spread(NZ, z, lambda p: gs.at[2], gzr.at[z], dev_z)
    gzr[z] = gs[2]

    landed(e_c)
    for k in range(3):
        for i in range(NL):
            at = pl.ds(pl.multiple_of((i * NC + c) * 128, 128), 128)
            both = efull[k, at, :] + er0[k, i].astype(F32)
            both = both.astype(BF)
            for j in range(NX):
                exs[j, k, i] = both[32 * j : 32 * j + 32]
    e_x = spread(NX, x, lambda p: exs.at[p], exr.at[x], dev_x)
    exr[x] = exs[x]

    landed(p_z)
    for i in range(NH):
        acc = azr[0, i].astype(F32)
        for j in range(1, NZ):
            acc = acc + azr[j, i].astype(F32)
        s2[NL * i] = acc[:8]
        s2[NL * i + 1] = acc[8:]
    p_y = spread(NY, y, lambda p: s2.at[p], ayr.at[y], dev_y)
    ayr[y] = s2[y]
    landed(g_z)
    acc = gzr[0]
    for j in range(1, NZ):
        acc = acc + gzr[j]
    gs[3] = acc
    g_y = spread(NY, y, lambda p: gs.at[3], gyr.at[y], dev_y)
    gyr[y] = gs[3]

    edge2.wait_recv()
    lext[pl.ds(FR, 8), :] = edge2_r[...].astype(F32)[:8]
    act_grad = None
    for k in range(3):
        w = (lext[pl.ds(k, FR), :] * back_masks[k]).astype(BF)
        term = dot(w, wenc[k], NT)
        act_grad = term if act_grad is None else act_grad + term
    feats = feat_ref[...].astype(F32)
    slope = jnp.where(feats > 0, 1.0, jnp.exp(feats))
    gf_ref[...] = (slope * act_grad).astype(BF)

    landed(e_x)
    for i in range(NL):
        for k in range(3):
            acc = exr[0, k, i].astype(F32)
            for j in range(1, NX):
                acc = acc + exr[j, k, i].astype(F32)
            for j in range(NZ):
                r, q = j // 2, j % 2
                ezs[j, i, k] = acc[8 * r : 8 * r + 8, 128 * q : 128 * q + 128].astype(BF)
    e_z = spread(NZ, z, lambda p: ezs.at[p], ezr.at[z], dev_z)
    ezr[z] = ezs[z]

    landed(p_y)
    acc = ayr[0]
    for j in range(1, NY):
        acc = acc + ayr[j]
    s3[...] = acc
    p_f = [push(s3, acr.at[c], dev_c(other))]
    acr[c] = s3[...]
    landed(g_y)
    acc = gyr[0]
    for j in range(1, NY):
        acc = acc + gyr[j]
    gg_ref[...] = acc

    landed(e_z)
    for i in range(NL):
        for k in range(3):
            acc = ezr[0, i, k].astype(F32)
            for j in range(1, NZ):
                acc = acc + ezr[j, i, k].astype(F32)
            eys[i, k] = acc.astype(BF)
    e_y = spread(NY, y, lambda p: eys.at[p % NL], eyr.at[y], dev_y)
    eyr[y] = eys[l]

    landed(p_f)
    low, high = acr[0], acr[1]
    both = jnp.concatenate([low, high], axis=1)
    gw_ref[...] = jnp.where(c == 0, both[:4], both[4:])

    landed(e_y)
    for k in range(3):
        acc = eyr[0, k].astype(F32)
        for j in range(1, NY):
            acc = acc + eyr[j, k].astype(F32)
        gz[z, k] = acc.astype(BF)
    mine_z = gz.at[z]
    o_z = spread(NZ, z, lambda p: mine_z, mine_z, dev_z)
    landed(o_z)
    o_x = spread(NX, x, lambda p: gz, gx.at[x], dev_x)
    gx[x] = gz[...]
    landed(o_x)
    for i in range(NX):
        for j in range(NZ):
            r, q = j // 2, j % 2
            for k in range(3):
                ge_ref[k, 32 * i + 8 * r : 32 * i + 8 * r + 8, 128 * q : 128 * q + 128] = gx[
                    i, j, k
                ].astype(F32)

    for copy in started:
        copy.wait_send()
    assert count[0] <= NSEM


def per_device(features, lengths, owner, w_enc, w_in, gain, cotangent):
    book = lax.axis_index("book")
    tall = jnp.tile(w_in.T, (4, 1))
    here = (jnp.arange(16, dtype=I32) // 4 == book)[:, None]
    padded = jnp.where(here, tall, jnp.zeros_like(tall))
    padded = padded.reshape(16, 2, 128).transpose(1, 0, 2)

    vmem = pl.BlockSpec(memory_space=pltpu.VMEM)
    anyspace = pl.BlockSpec(memory_space=pl.ANY)
    V = pltpu.VMEM
    scratch = [
        V((ROWS, DM), BF), V((3, CH, LAT), BF), V((8 + FR, CH), F32),
        V((16, CH), BF), V((16, CH), BF), V((3, FR, CH), BF),
        V((4, 16, 128), BF), V((2, NH, NZ, NX, 16, 128), BF),
        V((NX, NZ, 8, LAT), BF), V((NX, NZ, 8, LAT), BF), V((NZ, NX, 8, LAT), BF),
        V((NH, 64, LAT), BF), V((NH, 64, LAT), BF), V((2, ROWS, 128), BF),
        V((ROWS, DM), F32), V((ROWS, DM), BF),
        V((NH, 64, LAT), BF), V((NH, 64, LAT), BF), V((NZ, NX, 8, LAT), BF),
        V((NZ, NX, 8, LAT), BF), V((NX, NZ, 8, LAT), BF), V((FR + 8, LAT), F32),
        V((16, LAT), BF), V((16, LAT), BF),
        V((DM, 128), BF), V((DM, 128), BF), V((DM, 128), F32),
        V((NH, NZ, NX, 16, 128), BF), V((NX, NH, NZ, 16, 128), BF),
        V((NH, NZ, 16, 128), BF), V((NZ, NH, 16, 128), BF),
        V((NY, 8, 128), F32), V((NY, 8, 128), F32), V((8, 128), F32), V((2, 8, 128), F32),
        V((4, 1, DM), F32), V((NC, 1, DM), F32), V((NX, 1, DM), F32),
        V((NZ, 1, DM), F32), V((NY, 1, DM), F32), V((8, DM), F32),
        V((3, CH, LAT), F32), V((NC, 3, NL, 128, LAT), BF), V((3, NL, 128, LAT), BF),
        V((NX, 3, NL, 32, LAT), BF), V((NX, 3, NL, 32, LAT), BF),
        V((NZ, NL, 3, 8, 128), BF), V((NZ, NL, 3, 8, 128), BF),
        V((NL, 3, 8, 128), BF), V((NY, 3, 8, 128), BF),
        V((NZ, 3, 8, 128), BF), V((NX, NZ, 3, 8, 128), BF),
        pltpu.SemaphoreType.DMA((NSEM,)), pltpu.SemaphoreType.DMA((NSEM,)),
        pltpu.SemaphoreType.DMA((2,)),
    ]
    gf, ge, gw, gg = pl.pallas_call(
        kernel,
        out_shape=(
            jax.ShapeDtypeStruct((FR, CH), BF),
            jax.ShapeDtypeStruct((3, CH // 4, LAT), F32),
            jax.ShapeDtypeStruct((4, LAT), F32),
            jax.ShapeDtypeStruct((1, DM), F32),
        ),
        in_specs=[vmem, pl.BlockSpec(memory_space=pltpu.SMEM), vmem, vmem, vmem, anyspace, anyspace],
        out_specs=(vmem, vmem, vmem, vmem),
        scratch_shapes=scratch,
        compiler_params=pltpu.CompilerParams(
            collective_id=0, has_side_effects=True, vmem_limit_bytes=48 << 20
        ),
        name="encoder_back",
    )(
        features[0], lengths, owner.reshape(1, FR), padded, gain.reshape(1, DM),
        w_enc, cotangent[0],
    )
    return gf[None], ge, gw.T, gg.reshape(DM)


def solution(mesh):
    placed = (
        P("book", "seq", None),
        P("book", None),
        P("book", "seq", None),
        P(),
        P(None, ("seq", "book")),
        P(),
        P("book", "seq", None),
    )
    return jax.shard_map(
        per_device,
        mesh=mesh,
        in_specs=placed,
        out_specs=(P("book", "seq", None), P(None, "book", None), P(None, ("seq", "book")), P()),
        check_vma=False,
    )
```
